32 devices in a mesh: slide: 2 (over y), tile: 16 (over z, x, core).
Axes of the slice: x: 2, y: 2, z: 4, core: 2. Of those that a mesh axis runs over, the one named last changes fastest.
Arguments:
- fine_level: bfloat16 [2, 128, 256, 256], P('slide', 'tile'), may hold values from -6 to 6
- coarse_level: bfloat16 [2, 64, 128, 256], P('slide', 'tile'), may hold values from -6 to 6
- fine_kernel: bfloat16 [256, 9, 128], replicated, may hold values from -0.125 to 0.125
- coarse_kernel: bfloat16 [256, 9, 128], replicated, may hold values from -0.125 to 0.125
- fine_gain: float32 [128], replicated, may hold values from 0.25 to 1.75
- fine_offset: float32 [128], replicated, may hold values from -3 to 3
- coarse_gain: float32 [128], replicated, may hold values from 0.25 to 1.75
- coarse_offset: float32 [128], replicated, may hold values from -3 to 3
- class_kernel: bfloat16 [8, 128], replicated
- class_offset: float32 [8], replicated, may hold values from -4 to 4
- tissue_labels: int32 [2, 128, 256], P('slide', 'tile'), may hold values from -1 to 7, as said below
Outputs:
- loss: float32 [], replicated
- head_grads: float32 [12, 128], replicated
- conv_grads: float32 [256, 2, 9, 128], P('tile')
The draws below stay inside these ranges and needn't reach their ends.
Inputs may be any that keep to these rules, and one draw needn't show every extreme that they name: `tissue_labels`: -1 marks a pixel without tissue, other values are classes.
All inputs are finite; a program needn't handle non-finite values.
Results may differ from the reference program's by a relative error of at most 0.0033.
Values may be sent and summed in bfloat16 or wider, within the bound.
A program may use at most 128 MiB of HBM per device.

```python
import jax
import jax.numpy as jnp
from jax import lax

FPN_CH = 256
HEAD_CH = 128
GROUPS = 32
CLASSES = 8
COLS = 256
SLIDES = 2
ROWS = 128


def draw_class_kernel(key, part):
    first_key = jax.random.fold_in(jax.random.fold_in(key, 71), 0)
    base = jax.random.normal(first_key, (CLASSES, HEAD_CH), jnp.float32) / jnp.sqrt(jnp.float32(HEAD_CH))
    return base.astype(jnp.bfloat16)


def draw_tissue_labels(key, part):
    first_key, second_key = jax.random.split(jax.random.fold_in(key, 53))
    shape = (SLIDES, ROWS, COLS)
    draws = jax.random.randint(first_key, shape, 0, 1000, dtype=jnp.int32)
    classes = jax.random.randint(second_key, shape, 0, CLASSES, dtype=jnp.int32)
    row_index = lax.broadcasted_iota(jnp.int32, shape, 1)
    threshold = 250 + 500 * row_index // ROWS
    return jnp.where(draws < threshold, classes, -1).astype(jnp.int32)


def strengthened(result, stream_key, source, target, blocks, factor):
    def block_of(axis_at):
        return (jnp.arange(result.shape[axis_at]) // (result.shape[axis_at] // blocks)).reshape((-1,) + (1,) * (result.ndim - 1 - axis_at))

    one_side = jax.random.permutation(stream_key, blocks)[block_of(target)]
    other_side = (block_of(target) + blocks // 2) % blocks
    return jnp.where((block_of(source) == one_side) | (block_of(source) == other_side), factor * result, result)


def level_of(rng, extent, cuts, smallest, top_value):
    level = 1.0
    for axis_at, shards_of in cuts:
        steps = jax.random.uniform(jax.random.fold_in(jax.random.fold_in(rng, 6), axis_at), (shards_of,), jnp.float32, smallest / len(cuts), top_value / len(cuts))
        level = level * jnp.repeat(jnp.exp(steps), extent[axis_at] // shards_of).reshape((-1,) + (1,) * (len(extent) - 1 - axis_at))
    return level


def noise(stream_key, shape, scale, limit, cuts=(), kind=jnp.bfloat16):
    values = scale * jax.random.normal(stream_key, shape, jnp.float32)
    if cuts:
        values = values * level_of(stream_key, shape, cuts, -0.22, 0.18)
    return jnp.clip(values, -limit, limit).astype(kind)


def gaussian_with(key, extent, scale, limit, cuts, heavy, kind=jnp.bfloat16):
    entries = scale * jax.random.normal(key, extent, jnp.float32)
    if cuts:
        entries = entries * level_of(key, extent, cuts, -0.22, 0.18)
    return jnp.clip(strengthened(entries, jax.random.fold_in(key, 3), *heavy), -limit, limit).astype(kind)


def setup_inputs(seed: int = 0) -> dict:
    key_of = jax.random.split(jax.random.key(seed), 12)
    return {
        "fine_level": gaussian_with(key_of[0], (SLIDES, ROWS, COLS, FPN_CH), 1.0, 6.0, ((0, 2), (1, 16)), (1, 3, 16, 2.0)),
        "coarse_level": gaussian_with(key_of[1], (SLIDES, ROWS // 2, COLS // 2, FPN_CH), 1.0, 6.0, ((0, 2), (1, 16)), (1, 3, 16, 2.0)),
        "fine_kernel": noise(key_of[2], (FPN_CH, 9, HEAD_CH), (9 * FPN_CH) ** -0.5, 0.125),
        "coarse_kernel": noise(key_of[3], (FPN_CH, 9, HEAD_CH), (9 * FPN_CH) ** -0.5, 0.125),
        "fine_gain": jnp.clip(1.0 + 0.15 * jax.random.normal(key_of[4], (HEAD_CH,), jnp.float32), 0.25, 1.75),
        "fine_offset": noise(key_of[5], (HEAD_CH,), 0.5, 3.0, (), jnp.float32),
        "coarse_gain": jnp.clip(1.0 + 0.15 * jax.random.normal(key_of[6], (HEAD_CH,), jnp.float32), 0.25, 1.75),
        "coarse_offset": noise(key_of[7], (HEAD_CH,), 0.5, 3.0, (), jnp.float32),
        "class_kernel": draw_class_kernel(jax.random.fold_in(key_of[11], 71), 0),
        "class_offset": noise(key_of[9], (CLASSES,), 1.0, 4.0, (), jnp.float32),
        "tissue_labels": draw_tissue_labels(jax.random.fold_in(key_of[11], 71), 0),
    }


epsilon = 1e-05

def shifted(padded, height, width, position):
    row_step = position // 3
    col_step = position % 3
    return padded[row_step:row_step + height, col_step:col_step + width].reshape(height * width, -1)

def convolve(padded, kernel, height, width):
    total = jnp.zeros((height * width, kernel.shape[2]), jnp.float32)
    for position in range(9):
        total = total + jnp.dot(shifted(padded, height, width, position), kernel[:, position, :], preferred_element_type=jnp.float32)
    return total

def group_sums(values, groups):
    return values.reshape(values.shape[0], groups, -1).sum(axis=(0, 2))

def spread(per_group, channels):
    return jnp.repeat(per_group, channels // per_group.shape[0])

def kernel_grads(padded, upstream, height, width):
    taps = [lax.dot_general(shifted(padded, height, width, position), upstream, (((0,), (0,)), ((), ())), preferred_element_type=jnp.float32) for position in range(9)]
    return jnp.stack(taps, 1)

def one_slide(level_fine, level_coarse, labels, fine_kernel, coarse_kernel, fine_gain, fine_offset, coarse_gain, coarse_offset, class_kernel, class_offset, total):
    height, width = (level_fine.shape[0], level_fine.shape[1])
    channels = fine_kernel.shape[2]
    states = []
    for level, kernel, gain, offset in ((level_fine, fine_kernel, fine_gain, fine_offset), (level_coarse, coarse_kernel, coarse_gain, coarse_offset)):
        rows_here, cols_here = (level.shape[0], level.shape[1])
        padded = jnp.pad(level, ((1, 1), (1, 1), (0, 0)))
        conv_out = convolve(padded, kernel, rows_here, cols_here)
        number = rows_here * cols_here * (channels // GROUPS)
        mean = group_sums(conv_out, GROUPS) / number
        variance = group_sums(conv_out * conv_out, GROUPS) / number - mean * mean
        scale = spread(lax.rsqrt(variance + epsilon), channels)
        normed = (conv_out - spread(mean, channels)) * scale
        pre_act = normed * gain + offset
        states.append((padded, normed, scale, pre_act, gain, number, rows_here, cols_here))
    act_fine = jnp.maximum(states[0][3], 0.0).reshape(height, width, channels)
    act_coarse = jnp.maximum(states[1][3], 0.0).reshape(height // 2, width // 2, channels)
    upsampled = jnp.repeat(jnp.repeat(act_coarse, 2, 0), 2, 1)
    merged = (act_fine + upsampled).astype(jnp.bfloat16).reshape(height * width, channels)
    logits = lax.dot_general(class_kernel, merged, (((1,), (1,)), ((), ())), preferred_element_type=jnp.float32) + class_offset[:, None]
    flat_labels = labels.reshape(-1)
    tissue = (flat_labels >= 0).astype(jnp.float32)
    onehot = (flat_labels[None, :] == jnp.arange(CLASSES, dtype=jnp.int32)[:, None]).astype(jnp.float32)
    top = lax.optimization_barrier(jnp.max(logits, axis=0))
    lse = top + jnp.log(lax.optimization_barrier(jnp.sum(jnp.exp(logits - top[None, :]), axis=0)))
    loss_sum = jnp.sum((lse - lax.optimization_barrier(jnp.sum(onehot * logits, axis=0))) * tissue)
    dlogits = ((jnp.exp(logits - lse[None, :]) - onehot) * tissue[None, :] / total).astype(jnp.bfloat16)
    class_grad = jnp.dot(dlogits, merged, preferred_element_type=jnp.float32)
    dmerged = lax.dot_general(dlogits, class_kernel, (((0,), (0,)), ((), ())), preferred_element_type=jnp.float32)
    dact_fine = dmerged
    dact_coarse = dmerged.reshape(height // 2, 2, width // 2, 2, channels).sum(axis=(1, 3)).reshape(-1, channels)
    norm_rows = []
    conv_rows = []
    for state, upstream in ((states[0], dact_fine), (states[1], dact_coarse)):
        padded, normed, scale, pre_act, gain, number, rows_here, cols_here = state
        dpre = upstream * (pre_act > 0).astype(jnp.float32)
        norm_rows.append(lax.optimization_barrier(jnp.sum(dpre * normed, axis=0)))
        norm_rows.append(lax.optimization_barrier(jnp.sum(dpre, axis=0)))
        dnorm = dpre * gain
        first = spread(group_sums(dnorm, GROUPS) / number, channels)
        second = spread(group_sums(dnorm * normed, GROUPS) / number, channels)
        dconv = ((dnorm - first - normed * second) * scale).astype(jnp.bfloat16)
        conv_rows.append(kernel_grads(padded, dconv, rows_here, cols_here))
    head = jnp.concatenate([jnp.stack(norm_rows, 0), class_grad], 0)
    return (loss_sum, head, jnp.stack(conv_rows, 1))

def reference(fine_level, coarse_level, fine_kernel, coarse_kernel, fine_gain, fine_offset, coarse_gain, coarse_offset, class_kernel, class_offset, tissue_labels):
    total = jnp.sum((tissue_labels >= 0).astype(jnp.float32))

    def run(index):
        return one_slide(fine_level[index], coarse_level[index], tissue_labels[index], fine_kernel, coarse_kernel, fine_gain, fine_offset, coarse_gain, coarse_offset, class_kernel, class_offset, total)
    loss_sums, heads, convs = lax.map(run, jnp.arange(SLIDES, dtype=jnp.int32))
    return (jnp.sum(loss_sums) / total, lax.optimization_barrier(jnp.sum(heads, axis=0)), lax.optimization_barrier(jnp.sum(convs, axis=0)))
```

```python
import functools

import jax
import jax.numpy as jnp
from jax import lax
from jax.experimental import pallas as pl
from jax.experimental.pallas import tpu as pltpu
from jax.sharding import PartitionSpec as P

GROUPS = 32
EPSILON = 1e-05
F32 = jnp.float32
BF16 = jnp.bfloat16
MESH = pl.DeviceIdType.MESH
VMEM = pl.BlockSpec(memory_space=pltpu.VMEM)
LIMIT = 60 * 1024 * 1024
HIGH = lax.Precision.HIGHEST


def call(body, out_shape, scratch, args, collective_id=None):
    if collective_id is None:
        params = pltpu.CompilerParams(vmem_limit_bytes=LIMIT)
    else:
        params = pltpu.CompilerParams(
            vmem_limit_bytes=LIMIT, collective_id=collective_id, has_side_effects=True
        )
    return pl.pallas_call(
        body,
        out_shape=out_shape,
        in_specs=[VMEM] * len(args),
        out_specs=jax.tree.map(lambda _: VMEM, out_shape),
        scratch_shapes=scratch,
        compiler_params=params,
    )(*args)


def shape_of(dims, dtype=F32):
    return jax.ShapeDtypeStruct(dims, dtype)


def greet(peers):
    barrier = pltpu.get_barrier_semaphore()
    for peer in peers:
        pl.semaphore_signal(barrier, inc=1, device_id=peer, device_id_type=MESH)
    pl.semaphore_wait(barrier, len(peers))


def ring_peers(axis, size):
    me = lax.axis_index(axis)
    return [{axis: lax.rem(me + d, size)} for d in range(1, size)]


def spread_copies(axis, size, source, gather, send_sem, recv_sem):
    me = lax.axis_index(axis)
    return [
        pltpu.make_async_remote_copy(
            src_ref=source,
            dst_ref=gather.at[me],
            send_sem=send_sem.at[d - 1],
            recv_sem=recv_sem.at[d - 1],
            device_id={axis: lax.rem(me + d, size)},
            device_id_type=MESH,
        )
        for d in range(1, size)
    ]


def ordered_sum(gather, size):
    total = gather[0]
    for index in range(1, size):
        total = total + gather[index]
    return total


def dma_sems(*dims):
    return pltpu.SemaphoreType.DMA(dims)


def edge_kernel(tiles, fine, coarse, labels, fine_edge, coarse_edge, count_out,
                count, gather, down_send, down_recv, up_send, up_recv, send_sem, recv_sem):
    me = lax.axis_index("tile")
    tissue = (labels[...] >= 0).astype(F32)
    count[...] = jnp.broadcast_to(jnp.sum(tissue, axis=(0, 1), keepdims=True), count.shape)
    greet(ring_peers("tile", tiles))

    def edge_copies(peer, last, slot, send, recv):
        return [
            pltpu.make_async_remote_copy(
                src_ref=source.at[source.shape[0] - 1 if last else 0],
                dst_ref=target.at[slot],
                send_sem=send.at[at],
                recv_sem=recv.at[at],
                device_id={"tile": peer},
                device_id_type=MESH,
            )
            for at, (source, target) in enumerate(((fine, fine_edge), (coarse, coarse_edge)))
        ]

    down = edge_copies(lax.rem(me + 1, tiles), 1, 0, down_send, down_recv)
    up = edge_copies(lax.rem(me + tiles - 1, tiles), 0, 1, up_send, up_recv)

    @pl.when(me < tiles - 1)
    def _():
        for copy in down:
            copy.start()

    @pl.when(me > 0)
    def _():
        for copy in up:
            copy.start()

    copies = spread_copies("tile", tiles, count, gather, send_sem, recv_sem)
    for copy in copies:
        copy.start()
    gather[me] = count[...]

    @pl.when(me == 0)
    def _():
        fine_edge[0] = jnp.zeros(fine_edge.shape[1:], BF16)
        coarse_edge[0] = jnp.zeros(coarse_edge.shape[1:], BF16)

    @pl.when(me == tiles - 1)
    def _():
        fine_edge[1] = jnp.zeros(fine_edge.shape[1:], BF16)
        coarse_edge[1] = jnp.zeros(coarse_edge.shape[1:], BF16)

    for copy in copies:
        copy.wait()
    count_out[...] = ordered_sum(gather, tiles)

    @pl.when(me < tiles - 1)
    def _():
        for copy in down:
            copy.wait_send()
        for copy in up:
            copy.wait_recv()

    @pl.when(me > 0)
    def _():
        for copy in up:
            copy.wait_send()
        for copy in down:
            copy.wait_recv()


def pad_rows(level, edge, padded):
    rows = level.shape[0]
    padded[0] = edge[0]
    padded[pl.ds(1, rows)] = level[...]
    padded[rows + 1] = edge[1]


def column_of(shape, width):
    return lax.rem(lax.broadcasted_iota(jnp.int32, shape, 0), width)


def from_left(values, width):
    moved = pltpu.roll(values, 1, axis=0)
    return jnp.where(column_of(values.shape, width) == 0, 0.0, moved)


def from_right(values, width):
    moved = pltpu.roll(values, values.shape[0] - 1, axis=0)
    return jnp.where(column_of(values.shape, width) == width - 1, 0.0, moved)


def conv_kernel(fine, fine_edge, coarse, coarse_edge, fine_taps, coarse_taps,
                fine_conv, coarse_conv, stats, fine_pad, coarse_pad):
    pad_rows(fine, fine_edge, fine_pad)
    pad_rows(coarse, coarse_edge, coarse_pad)
    stats[...] = jnp.zeros_like(stats)
    for at, padded, taps, out in (
        (0, fine_pad, fine_taps, fine_conv),
        (2, coarse_pad, coarse_taps, coarse_conv),
    ):
        rows, width, depth = padded.shape[0] - 2, padded.shape[1], padded.shape[2]
        channels = taps.shape[2] // 3
        pack = 2
        size = pack * width

        @pl.loop(0, rows // pack)
        def _(step):
            total = None
            for a in range(3):
                block = padded[pl.ds(step * pack + a, pack)].reshape(size, depth)
                term = jnp.dot(block, taps[a], preferred_element_type=F32)
                total = term if total is None else total + term
            value = (
                from_left(total[:, :channels], width)
                + total[:, channels : 2 * channels]
                + from_right(total[:, 2 * channels :], width)
            )
            out[pl.ds(pl.multiple_of(step * size, size), size), :] = value
            stats[at : at + 1] += jnp.sum(value, axis=0, keepdims=True)
            stats[at + 1 : at + 2] += jnp.sum(value * value, axis=0, keepdims=True)


def stats_kernel(tiles, slides, local, count, out, total_out,
                 gather, count_gather, send_sem, recv_sem, slide_send, slide_recv):
    greet(ring_peers("tile", tiles) + ring_peers("slide", slides))
    copies = spread_copies("tile", tiles, local, gather, send_sem, recv_sem)
    others = spread_copies("slide", slides, count, count_gather, slide_send, slide_recv)
    for copy in copies + others:
        copy.start()
    gather[lax.axis_index("tile")] = local[...]
    count_gather[lax.axis_index("slide")] = count[...]
    for copy in copies + others:
        copy.wait()
    out[...] = ordered_sum(gather, tiles)
    total_out[...] = ordered_sum(count_gather, slides)


def group_total(rows, channels):
    width = channels // GROUPS
    first = lax.broadcasted_iota(jnp.int32, (channels, channels), 0) // width
    second = lax.broadcasted_iota(jnp.int32, (channels, channels), 1) // width
    same = (first == second).astype(F32)
    return jnp.dot(rows, same, preferred_element_type=F32, precision=HIGH)


def norm_terms(stats, numbers, channels):
    sums = group_total(stats[...], channels)
    terms = []
    for at, number in ((0, numbers[0]), (2, numbers[1])):
        mean = sums[at : at + 1] / number
        variance = sums[at + 1 : at + 2] / number - mean * mean
        terms.append((mean, lax.rsqrt(variance + EPSILON)))
    return terms


def head_kernel(numbers, width, fine_conv, coarse_conv, stats, norms, class_kernel,
                class_offset, labels, total, fine_dpre, coarse_dpre, rows, up, fold):
    channels = fine_conv.shape[1]
    classes = class_kernel.shape[0]
    (fine_mean, fine_scale), (coarse_mean, coarse_scale) = norm_terms(stats, numbers, channels)
    fine_gain, fine_offset = norms[0:1], norms[1:2]
    coarse_gain, coarse_offset = norms[2:3], norms[3:4]
    size, half = 2 * width, width // 2
    count = total[0:1, 0:1]
    rows[...] = jnp.zeros_like(rows)

    @pl.loop(0, fine_conv.shape[0] // size)
    def _(step):
        fine_at = pl.ds(pl.multiple_of(step * size, size), size)
        coarse_at = pl.ds(pl.multiple_of(step * half, half), half)
        fine_normed = (fine_conv[fine_at, :] - fine_mean) * fine_scale
        fine_pre = fine_normed * fine_gain + fine_offset
        coarse_normed = (coarse_conv[coarse_at, :] - coarse_mean) * coarse_scale
        coarse_pre = coarse_normed * coarse_gain + coarse_offset
        coarse_act = jnp.maximum(coarse_pre, 0.0)
        up[pl.ds(0, half, stride=2), :] = coarse_act
        up[pl.ds(1, half, stride=2), :] = coarse_act
        upsampled = up[...]
        merged = (
            jnp.maximum(fine_pre, 0.0) + jnp.concatenate([upsampled, upsampled], axis=0)
        ).astype(BF16)
        logits = (
            lax.dot_general(
                class_kernel[...], merged, (((1,), (1,)), ((), ())), preferred_element_type=F32
            )
            + class_offset[...]
        )
        label = labels[step]
        classes_of = lax.broadcasted_iota(jnp.int32, (classes, size), 0)
        onehot = (classes_of == label).astype(F32)
        tissue = (label >= 0).astype(F32)
        top = jnp.max(logits, axis=0, keepdims=True)
        lse = top + jnp.log(jnp.sum(jnp.exp(logits - top), axis=0, keepdims=True))
        picked = jnp.sum(onehot * logits, axis=0, keepdims=True)
        loss = jnp.sum((lse - picked) * tissue, axis=1, keepdims=True)
        dlogits = ((jnp.exp(logits - lse) - onehot) * tissue / count).astype(BF16)
        dmerged = lax.dot_general(
            dlogits, class_kernel[...], (((0,), (0,)), ((), ())), preferred_element_type=F32
        )
        fine_d = jnp.where(fine_pre > 0, dmerged, 0.0)
        fine_dpre[fine_at, :] = fine_d
        fold[...] = dmerged[:width] + dmerged[width:]
        blocks = fold[pl.ds(0, half, stride=2), :] + fold[pl.ds(1, half, stride=2), :]
        coarse_d = jnp.where(coarse_pre > 0, blocks, 0.0)
        coarse_dpre[coarse_at, :] = coarse_d
        rows[0:1] += jnp.sum(fine_d * fine_normed, axis=0, keepdims=True)
        rows[1:2] += jnp.sum(fine_d, axis=0, keepdims=True)
        rows[2:3] += jnp.sum(coarse_d * coarse_normed, axis=0, keepdims=True)
        rows[3:4] += jnp.sum(coarse_d, axis=0, keepdims=True)
        rows[4 : 4 + classes] += jnp.dot(dlogits, merged, preferred_element_type=F32)
        rows[4 + classes : 5 + classes] += jnp.broadcast_to(loss, (1, channels))


def rows_kernel(tiles, local, out, gather, send_sem, recv_sem):
    greet(ring_peers("tile", tiles))
    copies = spread_copies("tile", tiles, local, gather, send_sem, recv_sem)
    for copy in copies:
        copy.start()
    gather[lax.axis_index("tile")] = local[...]
    for copy in copies:
        copy.wait()
    out[...] = ordered_sum(gather, tiles)


def grad_kernel(numbers, fine, fine_edge, coarse, coarse_edge, fine_conv, coarse_conv, stats,
                norms, rows, fine_dpre, coarse_dpre, fine_out, coarse_out, fine_pad, coarse_pad):
    channels = fine_conv.shape[1]
    terms = norm_terms(stats, numbers, channels)
    pad_rows(fine, fine_edge, fine_pad)
    pad_rows(coarse, coarse_edge, coarse_pad)
    gains = jnp.concatenate([norms[0:1], norms[0:1], norms[2:3], norms[2:3]], axis=0)
    back = group_total(
        jnp.concatenate([rows[0:4] * gains, jnp.zeros((4, channels), F32)], axis=0), channels
    )
    for at, padded, conv, dpre, out in (
        (2, coarse_pad, coarse_conv, coarse_dpre, coarse_out),
        (0, fine_pad, fine_conv, fine_dpre, fine_out),
    ):
        number = numbers[at // 2]
        mean, scale = terms[at // 2]
        gain = norms[at : at + 1]
        first = back[at + 1 : at + 2] / number
        second = back[at : at + 1] / number
        height, width, depth = padded.shape[0] - 2, padded.shape[1], padded.shape[2]
        pack = 2
        size = pack * width
        out[...] = jnp.zeros_like(out)
        lead = out.shape[:-1]

        @pl.loop(0, height // pack)
        def _(step):
            here = pl.ds(pl.multiple_of(step * size, size), size)
            normed = (conv[here, :] - mean) * scale
            dconv = (dpre[here, :] * gain - first - normed * second) * scale
            moved = jnp.concatenate(
                [
                    from_right(dconv, width).astype(BF16),
                    dconv.astype(BF16),
                    from_left(dconv, width).astype(BF16),
                ],
                axis=1,
            )
            for a in range(3):
                block = padded[pl.ds(step * pack + a, pack)].reshape(size, depth)
                term = lax.dot_general(
                    block, moved, (((0,), (0,)), ((), ())), preferred_element_type=F32
                )
                at_lanes = (slice(None),) * len(lead) + (
                    slice(a * 3 * channels, (a + 1) * 3 * channels),
                )
                out[at_lanes] += term.reshape(lead + (3 * channels,))


def orders_of(bits):
    first = list(range(bits))
    second = list(first)
    if bits > 2:
        second[1], second[2] = second[2], second[1]
    return first, second


def stage_plan(bits, order):
    left = list(reversed(range(bits)))
    plan = []
    for bit in order:
        place = left.index(bit)
        left = [other for other in left if other != bit]
        plan.append((bit, place, len(left)))
    return plan


def at_bits(places, count):
    index = [slice(None)] * count
    for place, value in places:
        index[place] = value
    return tuple(index)


def scatter_kernel(bits, slides, channels, *refs):
    fine, coarse, rows, out, head = refs[:5]
    fine_bufs = refs[5 : 5 + 3 * bits]
    coarse_bufs = refs[5 + 3 * bits : 5 + 6 * bits]
    (final, head_gather, send_sem, recv_sem, slide_send, slide_recv) = refs[5 + 6 * bits :]
    me, slide = lax.axis_index("tile"), lax.axis_index("slide")
    mine = [lax.rem(me // (2**bit), 2) for bit in range(bits)]
    partners = [{"tile": me + (1 - 2 * mine[bit]) * (2**bit)} for bit in range(bits)]
    greet(partners + ring_peers("slide", slides))
    plans = [stage_plan(bits, order) for order in orders_of(bits)]
    bufs = [fine_bufs, coarse_bufs]

    heads = spread_copies("slide", slides, rows, head_gather, slide_send.at[2], slide_recv.at[2])
    for copy in heads:
        copy.start()

    def stage_copy(level, stage):
        bit, place, left = plans[level][stage]
        if stage == 0:
            source = (fine, coarse)[level].at[at_bits([(place, 1 - mine[bit])], left + 1)]
        else:
            source = bufs[level][3 * stage + 1]
        return pltpu.make_async_remote_copy(
            src_ref=source,
            dst_ref=bufs[level][3 * stage + 2],
            send_sem=send_sem.at[level, stage],
            recv_sem=recv_sem.at[level, stage],
            device_id=partners[bit],
            device_id_type=MESH,
        )

    def slide_copies(level):
        return spread_copies(
            "slide", slides, final.at[level, slide], final.at[level],
            slide_send.at[level], slide_recv.at[level],
        )

    both = (1, 0)
    for level in both:
        stage_copy(level, 0).start()
    for stage in range(bits):
        for level in both:
            bit, place, left = plans[level][stage]
            stage_copy(level, stage).wait()
            if stage == 0:
                kept = (fine, coarse)[level].at[at_bits([(place, mine[bit])], left + 1)]
            else:
                kept = bufs[level][3 * stage]
            came = bufs[level][3 * stage + 2]
            if stage == bits - 1:
                final[level, slide] = kept[...] + came[...].astype(F32)
                for copy in slide_copies(level):
                    copy.start()
                continue
            later, spot, _ = plans[level][stage + 1]

            def part(value):
                chosen = at_bits([(spot, value)], left)
                return kept[chosen] + came[chosen].astype(F32)

            outgoing = bufs[level][3 * stage + 4]
            outgoing[...] = part(1 - mine[later]).astype(outgoing.dtype)
            stage_copy(level, stage + 1).start()
            bufs[level][3 * stage + 3][...] = part(mine[later])

    head_gather[slide] = rows[...]
    for copy in heads:
        copy.wait()
    head[...] = ordered_sum(head_gather, slides)
    for level in both:
        for copy in slide_copies(level):
            copy.wait()
        whole = final[level, 0]
        for index in range(1, slides):
            whole = whole + final[level, index]
        for tap in range(9):
            out[:, level, tap, :] = whole[:, tap * channels : (tap + 1) * channels]


def scatter_scratch(bits, slides, depth, width, rows_shape):
    scratch = []
    for order in orders_of(bits):
        for stage, (_, _, left) in enumerate(stage_plan(bits, order)):
            wire = F32 if stage == 0 else BF16
            below = (2,) * left + (depth, width)
            if stage == 0:
                tiny = (8, 128)
                scratch += [pltpu.VMEM(tiny, F32), pltpu.VMEM(tiny, F32)]
            else:
                scratch += [pltpu.VMEM(below, F32), pltpu.VMEM(below, wire)]
            scratch += [pltpu.VMEM(below, wire)]
    ends = max(slides - 1, 1)
    return scratch + [
        pltpu.VMEM((2, slides, depth, width), F32),
        pltpu.VMEM((slides,) + rows_shape, F32),
        dma_sems(2, bits),
        dma_sems(2, bits),
        dma_sems(3, ends),
        dma_sems(3, ends),
    ]


def per_device(
    fine_level,
    coarse_level,
    fine_kernel,
    coarse_kernel,
    fine_gain,
    fine_offset,
    coarse_gain,
    coarse_offset,
    class_kernel,
    class_offset,
    tissue_labels,
):
    tiles, slides = lax.axis_size("tile"), lax.axis_size("slide")
    bits = tiles.bit_length() - 1
    in_channels, _, channels = fine_kernel.shape
    classes = class_kernel.shape[0]
    fine, coarse, labels = fine_level[0], coarse_level[0], tissue_labels[0]
    height, width = fine.shape[0], fine.shape[1]
    fine_number = height * tiles * width * (channels // GROUPS)
    numbers = (float(fine_number), float(fine_number // 4))
    ends = tiles - 1

    def tap_rows(kernel):
        return kernel.reshape(in_channels, 3, 3 * channels).transpose(1, 0, 2)

    fine_edge, coarse_edge, count = call(
        functools.partial(edge_kernel, tiles),
        (
            shape_of((2,) + fine.shape[1:], BF16),
            shape_of((2,) + coarse.shape[1:], BF16),
            shape_of((1, channels)),
        ),
        [
            pltpu.VMEM((1, channels), F32),
            pltpu.VMEM((tiles, 1, channels), F32),
            dma_sems(2),
            dma_sems(2),
            dma_sems(2),
            dma_sems(2),
            dma_sems(ends),
            dma_sems(ends),
        ],
        (fine, coarse, labels),
        0,
    )
    pads = [
        pltpu.VMEM((height + 2, width, in_channels), BF16),
        pltpu.VMEM((height // 2 + 2, width // 2, in_channels), BF16),
    ]
    pixels = height * width
    fine_conv, coarse_conv, local = call(
        conv_kernel,
        (
            shape_of((pixels, channels)),
            shape_of((pixels // 4, channels)),
            shape_of((8, channels)),
        ),
        pads,
        (fine, fine_edge, coarse, coarse_edge, tap_rows(fine_kernel), tap_rows(coarse_kernel)),
    )
    stats, total = call(
        functools.partial(stats_kernel, tiles, slides),
        (shape_of((8, channels)), shape_of((1, channels))),
        [
            pltpu.VMEM((tiles, 8, channels), F32),
            pltpu.VMEM((slides, 1, channels), F32),
            dma_sems(ends),
            dma_sems(ends),
            dma_sems(max(slides - 1, 1)),
            dma_sems(max(slides - 1, 1)),
        ],
        (local, count),
        1,
    )
    norms = jnp.stack([fine_gain, fine_offset, coarse_gain, coarse_offset], 0)
    row_count = -(-(5 + classes) // 8) * 8
    fine_dpre, coarse_dpre, rows_local = call(
        functools.partial(head_kernel, numbers, width),
        (
            shape_of((pixels, channels)),
            shape_of((pixels // 4, channels)),
            shape_of((row_count, channels)),
        ),
        [pltpu.VMEM((width, channels), F32), pltpu.VMEM((width, channels), F32)],
        (
            fine_conv,
            coarse_conv,
            stats,
            norms,
            class_kernel,
            class_offset[:, None],
            labels.reshape(height // 2, 1, 2 * width),
            total,
        ),
    )
    rows = call(
        functools.partial(rows_kernel, tiles),
        shape_of((row_count, channels)),
        [pltpu.VMEM((tiles, row_count, channels), F32), dma_sems(ends), dma_sems(ends)],
        (rows_local,),
        2,
    )
    chunk = in_channels // tiles
    grads_shape = shape_of((2,) * bits + (chunk, 9 * channels))
    fine_grad, coarse_grad = call(
        functools.partial(grad_kernel, numbers),
        (grads_shape, grads_shape),
        pads,
        (
            fine,
            fine_edge,
            coarse,
            coarse_edge,
            fine_conv,
            coarse_conv,
            stats,
            norms,
            rows,
            fine_dpre,
            coarse_dpre,
        ),
    )
    conv_grads, head = call(
        functools.partial(scatter_kernel, bits, slides, channels),
        (shape_of((chunk, 2, 9, channels)), shape_of((row_count, channels))),
        scatter_scratch(bits, slides, chunk, 9 * channels, (row_count, channels)),
        (fine_grad, coarse_grad, rows),
        3,
    )
    return (head[4 + classes, 0] / total[0, 0], head[: 4 + classes], conv_grads)


def solution(mesh):
    return jax.shard_map(
        per_device,
        mesh=mesh,
        in_specs=(
            P("slide", "tile", None, None),
            P("slide", "tile", None, None),
            P(),
            P(),
            P(),
            P(),
            P(),
            P(),
            P(),
            P(),
            P("slide", "tile", None),
        ),
        out_specs=(P(), P(), P("tile", None, None, None)),
        check_vma=False,
    )
```

```python
import functools
import types

import jax
import jax.numpy as jnp
from jax import lax
from jax.experimental import pallas as pl
from jax.experimental.pallas import tpu as pltpu
from jax.sharding import PartitionSpec as P

GROUPS = 32
EPSILON = 1e-05
F32 = jnp.float32
BF16 = jnp.bfloat16
MESH = pl.DeviceIdType.MESH
VMEM = pl.BlockSpec(memory_space=pltpu.VMEM)
LIMIT = 60 * 1024 * 1024
HIGH = lax.Precision.HIGHEST


def call(body, out_shape, scratch, args, collective_id=None):
    if collective_id is None:
        params = pltpu.CompilerParams(vmem_limit_bytes=LIMIT)
    else:
        params = pltpu.CompilerParams(
            vmem_limit_bytes=LIMIT, collective_id=collective_id, has_side_effects=True
        )
    return pl.pallas_call(
        body,
        out_shape=out_shape,
        in_specs=[VMEM] * len(args),
        out_specs=jax.tree.map(lambda _: VMEM, out_shape),
        scratch_shapes=scratch,
        compiler_params=params,
    )(*args)


def shape_of(dims, dtype=F32):
    return jax.ShapeDtypeStruct(dims, dtype)


def greet(peers):
    barrier = pltpu.get_barrier_semaphore()
    for peer in peers:
        pl.semaphore_signal(barrier, inc=1, device_id=peer, device_id_type=MESH)
    pl.semaphore_wait(barrier, len(peers))


def ring_peers(axis, size):
    me = lax.axis_index(axis)
    return [{axis: lax.rem(me + d, size)} for d in range(1, size)]


def spread_copies(axis, size, source, gather, send_sem, recv_sem):
    me = lax.axis_index(axis)
    return [
        pltpu.make_async_remote_copy(
            src_ref=source,
            dst_ref=gather.at[me],
            send_sem=send_sem.at[d - 1],
            recv_sem=recv_sem.at[d - 1],
            device_id={axis: lax.rem(me + d, size)},
            device_id_type=MESH,
        )
        for d in range(1, size)
    ]


def ordered_sum(gather, size):
    total = gather[0]
    for index in range(1, size):
        total = total + gather[index]
    return total


def dma_sems(*dims):
    return pltpu.SemaphoreType.DMA(dims)


def column_of(shape, width):
    return lax.rem(lax.broadcasted_iota(jnp.int32, shape, 0), width)


def from_left(values, width):
    moved = pltpu.roll(values, 1, axis=0)
    return jnp.where(column_of(values.shape, width) == 0, 0.0, moved)


def from_right(values, width):
    moved = pltpu.roll(values, values.shape[0] - 1, axis=0)
    return jnp.where(column_of(values.shape, width) == width - 1, 0.0, moved)


def stage_plan(bits, order):
    left = list(reversed(range(bits)))
    plan = []
    for bit in order:
        place = left.index(bit)
        left = [other for other in left if other != bit]
        plan.append((bit, place, len(left)))
    return plan


def at_bits(places, count):
    index = [slice(None)] * count
    for place, value in places:
        index[place] = value
    return tuple(index)


def order_of(bits, turn):
    order = list(range(bits))
    if turn and bits > 2:
        order[1], order[2] = order[2], order[1]
    return order


def lanes_of(shape, dim=1):
    return lax.broadcasted_iota(jnp.int32, shape, dim)


def packed_groups(rows, channels):
    shape = (channels, channels)
    member = lanes_of(shape, 0) // (channels // GROUPS) == lax.rem(lanes_of(shape), GROUPS)
    sums = jnp.dot(rows, member.astype(F32), preferred_element_type=F32, precision=HIGH)
    own = lanes_of(rows.shape) // GROUPS == lanes_of(rows.shape, 0)
    return jnp.sum(jnp.where(own, sums, 0.0), axis=0, keepdims=True)


def unpacked_groups(row, channels):
    shape = (channels, channels)
    member = lax.rem(lanes_of(shape, 0), GROUPS) == lanes_of(shape) // (channels // GROUPS)
    own = lanes_of((8, channels)) // GROUPS == lanes_of((8, channels), 0)
    rows = jnp.where(own, jnp.broadcast_to(row, (8, channels)), 0.0)
    return jnp.dot(rows, member.astype(F32), preferred_element_type=F32, precision=HIGH)


PACK = 2
GRAD, SEND, RECV, KEPT = range(4)


def conv_step(step, padded, taps, out, sums, at):
    width, depth = padded.shape[1], padded.shape[2]
    channels = taps.shape[2]
    size = PACK * width
    total = None
    for a in range(3):
        block = padded[pl.ds(step * PACK + a, PACK)].reshape(size, depth)
        side = jnp.concatenate([taps[3 * a + b] for b in range(3)], axis=1)
        term = jnp.dot(block, side, preferred_element_type=F32)
        total = term if total is None else total + term
    value = (
        from_left(total[:, :channels], width)
        + total[:, channels : 2 * channels]
        + from_right(total[:, 2 * channels :], width)
    )
    here = step * size if isinstance(step, int) else pl.multiple_of(step * size, size)
    out[pl.ds(here, size), :] = value
    sums[at : at + 1] += jnp.sum(value, axis=0, keepdims=True)
    sums[at + 1 : at + 2] += jnp.sum(value * value, axis=0, keepdims=True)


def step_kernel(tiles, slides, bits, numbers, names, keys, *refs):
    ref = types.SimpleNamespace(**dict(zip(names, refs)))
    ref.parts = dict(zip(keys, refs[len(names) :]))
    fine, coarse, labels = ref.fine, ref.coarse, ref.labels
    fine_pad, coarse_pad = ref.fine_pad, ref.coarse_pad
    fine_conv, coarse_conv = ref.fine_conv, ref.coarse_conv
    sums, rows, class_kernel = ref.sums, ref.rows, ref.class_kernel
    me, slide = lax.axis_index("tile"), lax.axis_index("slide")
    height, width, _ = fine.shape
    channels = fine_conv.shape[1]
    classes = class_kernel.shape[0]
    fine_gain, fine_offset = ref.fine_gain[...], ref.fine_offset[...]
    coarse_gain, coarse_offset = ref.coarse_gain[...], ref.coarse_offset[...]

    tissue_here = (labels[...] >= 0).astype(F32)
    ref.count[...] = jnp.broadcast_to(
        jnp.sum(tissue_here, axis=(0, 1), keepdims=True), ref.count.shape
    )
    greet(ring_peers("tile", tiles) + ring_peers("slide", slides))

    def edge_copies(peer, down):
        return [
            pltpu.make_async_remote_copy(
                src_ref=source.at[source.shape[0] - 1 if down else 0],
                dst_ref=target.at[0 if down else target.shape[0] - 1],
                send_sem=ref.edge_send.at[int(down), at],
                recv_sem=ref.edge_recv.at[int(down), at],
                device_id={"tile": peer},
                device_id_type=MESH,
            )
            for at, (source, target) in enumerate(((fine, fine_pad), (coarse, coarse_pad)))
        ]

    down = edge_copies(lax.rem(me + 1, tiles), True)
    up = edge_copies(lax.rem(me + tiles - 1, tiles), False)

    @pl.when(me < tiles - 1)
    def _():
        for copy in down:
            copy.start()

    @pl.when(me > 0)
    def _():
        for copy in up:
            copy.start()

    def tile_copies(at, source, gather):
        return spread_copies(
            "tile", tiles, source, gather, ref.tile_send.at[at], ref.tile_recv.at[at]
        )

    def slide_copies(at, source, gather):
        return spread_copies(
            "slide", slides, source, gather, ref.slide_send.at[at], ref.slide_recv.at[at]
        )

    def start(copies):
        for copy in copies:
            copy.start()

    def wait(copies):
        for copy in copies:
            copy.wait()

    counts = tile_copies(0, ref.count, ref.count_gather)
    start(counts)
    ref.count_gather[me] = ref.count[...]

    @pl.when(me == 0)
    def _():
        for padded in (fine_pad, coarse_pad):
            padded[0] = jnp.zeros(padded.shape[1:], BF16)

    @pl.when(me == tiles - 1)
    def _():
        for padded in (fine_pad, coarse_pad):
            padded[padded.shape[0] - 1] = jnp.zeros(padded.shape[1:], BF16)

    sums[...] = jnp.zeros_like(sums)
    fine_pad[pl.ds(1, height)] = fine[...]
    coarse_pad[pl.ds(1, height // 2)] = coarse[...]
    fine_steps, coarse_steps = height // PACK, height // 2 // PACK

    @pl.loop(1, fine_steps - 1)
    def _(step):
        conv_step(step, fine_pad, ref.fine_taps, fine_conv, sums, 0)

    @pl.when(me < tiles - 1)
    def _():
        for copy in down:
            copy.wait_send()
        for copy in up:
            copy.wait_recv()

    @pl.when(me > 0)
    def _():
        for copy in up:
            copy.wait_send()
        for copy in down:
            copy.wait_recv()

    @pl.loop(0, 2)
    def _(side):
        conv_step(side * (fine_steps - 1), fine_pad, ref.fine_taps, fine_conv, sums, 0)

    @pl.loop(0, coarse_steps)
    def _(step):
        conv_step(step, coarse_pad, ref.coarse_taps, coarse_conv, sums, 2)

    ref.stat[...] = packed_groups(sums[...], channels)
    stat_copies = tile_copies(1, ref.stat, ref.stat_gather)
    start(stat_copies)
    wait(counts)
    ref.slide_count[...] = ordered_sum(ref.count_gather, tiles)
    total_copies = slide_copies(0, ref.slide_count, ref.total_gather)
    start(total_copies)
    ref.stat_gather[me] = ref.stat[...]
    ref.total_gather[slide] = ref.slide_count[...]

    for padded, turned in ((fine_pad, ref.fine_turned), (coarse_pad, ref.coarse_turned)):
        span = padded.shape[1]
        for row in range(padded.shape[0]):
            turned[:, row * span : (row + 1) * span] = padded[row].T

    wait(stat_copies)
    wait(total_copies)
    total = ordered_sum(ref.total_gather, slides)
    count = total[0:1, 0:1]
    ref.total_out[...] = total
    group_sums = unpacked_groups(ordered_sum(ref.stat_gather, tiles), channels)

    def terms_of(at, number):
        mean = group_sums[at : at + 1] / number
        variance = group_sums[at + 1 : at + 2] / number - mean * mean
        return mean, lax.rsqrt(variance + EPSILON)

    fine_mean, fine_scale = terms_of(0, numbers[0])
    coarse_mean, coarse_scale = terms_of(2, numbers[1])

    size, half = 2 * width, width // 2
    square = (classes, classes)
    offset = jnp.sum(
        jnp.where(
            lanes_of(square) == lanes_of(square, 0),
            jnp.broadcast_to(ref.class_offset[...], square),
            0.0,
        ),
        axis=1,
        keepdims=True,
    )
    rows[...] = jnp.zeros_like(rows)
    widen, fold = ref.widen, ref.fold
    fine_dpre, coarse_dpre = ref.fine_dpre, ref.coarse_dpre

    @pl.loop(0, height // 2)
    def _(step):
        fine_at = pl.ds(pl.multiple_of(step * size, size), size)
        coarse_at = pl.ds(pl.multiple_of(step * half, half), half)
        fine_normed = (fine_conv[fine_at, :] - fine_mean) * fine_scale
        fine_pre = fine_normed * fine_gain + fine_offset
        coarse_normed = (coarse_conv[coarse_at, :] - coarse_mean) * coarse_scale
        coarse_pre = coarse_normed * coarse_gain + coarse_offset
        coarse_act = jnp.maximum(coarse_pre, 0.0)
        widen[pl.ds(0, half, stride=2), :] = coarse_act
        widen[pl.ds(1, half, stride=2), :] = coarse_act
        upsampled = widen[...]
        merged = (
            jnp.maximum(fine_pre, 0.0) + jnp.concatenate([upsampled, upsampled], axis=0)
        ).astype(BF16)
        logits = (
            lax.dot_general(
                class_kernel[...], merged, (((1,), (1,)), ((), ())), preferred_element_type=F32
            )
            + offset
        )
        label = jnp.concatenate(
            [labels[pl.ds(2 * step, 1), :], labels[pl.ds(2 * step + 1, 1), :]], axis=1
        )
        onehot = (lanes_of((classes, size), 0) == label).astype(F32)
        tissue = (label >= 0).astype(F32)
        top = jnp.max(logits, axis=0, keepdims=True)
        lse = top + jnp.log(jnp.sum(jnp.exp(logits - top), axis=0, keepdims=True))
        picked = jnp.sum(onehot * logits, axis=0, keepdims=True)
        loss = jnp.sum((lse - picked) * tissue, axis=1, keepdims=True)
        dlogits = ((jnp.exp(logits - lse) - onehot) * tissue / count).astype(BF16)
        dmerged = lax.dot_general(
            dlogits, class_kernel[...], (((0,), (0,)), ((), ())), preferred_element_type=F32
        )
        fine_d = jnp.where(fine_pre > 0, dmerged, 0.0)
        fine_dpre[fine_at, :] = fine_d
        fold[...] = dmerged[:width] + dmerged[width:]
        blocks = fold[pl.ds(0, half, stride=2), :] + fold[pl.ds(1, half, stride=2), :]
        coarse_d = jnp.where(coarse_pre > 0, blocks, 0.0)
        coarse_dpre[coarse_at, :] = coarse_d
        rows[0:1] += jnp.sum(fine_d * fine_normed, axis=0, keepdims=True)
        rows[1:2] += jnp.sum(fine_d, axis=0, keepdims=True)
        rows[2:3] += jnp.sum(coarse_d * coarse_normed, axis=0, keepdims=True)
        rows[3:4] += jnp.sum(coarse_d, axis=0, keepdims=True)
        rows[4 : 4 + classes] += jnp.dot(dlogits, merged, preferred_element_type=F32)
        rows[4 + classes : 5 + classes] += jnp.broadcast_to(loss, (1, channels))

    gains = jnp.concatenate([fine_gain, fine_gain, coarse_gain, coarse_gain] * 2, axis=0)
    ref.back[...] = packed_groups(rows[0:8] * gains, channels)
    back_copies = tile_copies(2, ref.back, ref.back_gather)
    start(back_copies)
    row_copies = tile_copies(3, rows, ref.row_gather)
    start(row_copies)
    ref.back_gather[me] = ref.back[...]
    ref.row_gather[me] = rows[...]
    wait(back_copies)
    back = unpacked_groups(ordered_sum(ref.back_gather, tiles), channels)

    def upstream(conv, dpre, mean, scale, gain, at, number, span, shifted, steps):
        first = back[at + 1 : at + 2] / number
        second = back[at : at + 1] / number
        block = PACK * span

        @pl.loop(0, steps)
        def _(step):
            here = pl.ds(pl.multiple_of(step * block, block), block)
            normed = (conv[here, :] - mean) * scale
            dconv = (dpre[here, :] * gain - first - normed * second) * scale
            shifted[here, :] = jnp.concatenate(
                [
                    from_right(dconv, span).astype(BF16),
                    dconv.astype(BF16),
                    from_left(dconv, span).astype(BF16),
                ],
                axis=1,
            )

    mine = [lax.rem(me // (2**bit), 2) for bit in range(bits)]
    partners = [{"tile": me + (1 - 2 * mine[bit]) * (2**bit)} for bit in range(bits)]
    plans = [stage_plan(bits, order_of(bits, piece % 2 == 0)) for piece in range(4)]
    final = ref.final
    total_taps = 9 * channels
    spans = [(total_taps, total_taps)] + [(a * 3 * channels, 3 * channels) for a in range(3)]

    def buffer(piece, stage, kind):
        return ref.parts[kind, piece, stage]

    def stage_copy(piece, stage):
        bit, place, left = plans[piece][stage]
        if stage == 0:
            source = ref.parts[GRAD, piece, 0].at[at_bits([(place, 1 - mine[bit])], left + 1)]
        else:
            source = buffer(piece, stage, SEND)
        return pltpu.make_async_remote_copy(
            src_ref=source,
            dst_ref=buffer(piece, stage, RECV),
            send_sem=ref.stage_send.at[piece, stage],
            recv_sem=ref.stage_recv.at[piece, stage],
            device_id=partners[bit],
            device_id_type=MESH,
        )

    def piece_copies(piece):
        lanes = pl.ds(*spans[piece])
        return [
            pltpu.make_async_remote_copy(
                src_ref=final.at[slide, :, lanes],
                dst_ref=final.at[slide, :, lanes],
                send_sem=ref.slide_send.at[2 + piece, d - 1],
                recv_sem=ref.slide_recv.at[2 + piece, d - 1],
                device_id={"slide": lax.rem(slide + d, slides)},
                device_id_type=MESH,
            )
            for d in range(1, slides)
        ]

    done = [0] * 4

    def advance(piece):
        stage = done[piece]
        if stage == bits:
            return
        done[piece] += 1
        bit, place, left = plans[piece][stage]
        stage_copy(piece, stage).wait()
        if stage == 0:
            kept = ref.parts[GRAD, piece, 0].at[at_bits([(place, mine[bit])], left + 1)]
        else:
            kept = buffer(piece, stage, KEPT)
        came = buffer(piece, stage, RECV)
        if stage == bits - 1:
            final[slide, :, pl.ds(*spans[piece])] = kept[...] + came[...].astype(F32)
            start(piece_copies(piece))
            return
        later, spot, _ = plans[piece][stage + 1]

        def part(value):
            chosen = at_bits([(spot, value)], left)
            return kept[chosen] + came[chosen].astype(F32)

        buffer(piece, stage + 1, SEND)[...] = part(1 - mine[later]).astype(BF16)
        stage_copy(piece, stage + 1).start()
        buffer(piece, stage + 1, KEPT)[...] = part(mine[later])

    def product(turned, shifted, a, span):
        pixels = shifted.shape[0]
        return jnp.dot(
            turned[:, a * span : a * span + pixels], shifted[...], preferred_element_type=F32
        )

    coarse_shifted, fine_shifted = ref.coarse_shifted, ref.fine_shifted
    upstream(coarse_conv, coarse_dpre, coarse_mean, coarse_scale, coarse_gain, 2, numbers[1],
             half, coarse_shifted, coarse_steps)
    lead = (slice(None),) * (bits + 1)
    for a in range(3):
        value = product(ref.coarse_turned, coarse_shifted, a, half)
        out = ref.parts[GRAD, 0, 0]
        out[lead + (slice(a * 3 * channels, (a + 1) * 3 * channels),)] = value.reshape(
            out.shape[:-1] + (3 * channels,)
        )
    stage_copy(0, 0).start()
    upstream(fine_conv, fine_dpre, fine_mean, fine_scale, fine_gain, 0, numbers[0],
             width, fine_shifted, fine_steps)
    for a in range(3):
        out = ref.parts[GRAD, a + 1, 0]
        out[...] = product(ref.fine_turned, fine_shifted, a, width).reshape(out.shape)
        stage_copy(a + 1, 0).start()
        if a < 2:
            for piece in range(a + 1):
                advance(piece)
    wait(row_copies)
    ref.slide_rows[...] = ordered_sum(ref.row_gather, tiles)
    head_copies = slide_copies(1, ref.slide_rows, ref.head_gather)
    start(head_copies)
    ref.head_gather[slide] = ref.slide_rows[...]
    while min(done) < bits:
        for piece in range(4):
            advance(piece)
    wait(head_copies)
    for piece in range(4):
        wait(piece_copies(piece))


def finish_kernel(slides, classes, final, heads, total, loss, head, grads):
    channels = head.shape[1]
    whole = ordered_sum(final, slides)
    for level in range(2):
        for tap in range(9):
            at = (9 * level + tap) * channels
            grads[:, tap, level, :] = whole[:, at : at + channels]
    rows = ordered_sum(heads, slides)
    head[...] = rows[: 4 + classes]
    loss[...] = rows[4 + classes : 5 + classes, 0:1] / total[0:1, 0:1]


def per_device(
    fine_level,
    coarse_level,
    fine_kernel,
    coarse_kernel,
    fine_gain,
    fine_offset,
    coarse_gain,
    coarse_offset,
    class_kernel,
    class_offset,
    tissue_labels,
):
    tiles, slides = lax.axis_size("tile"), lax.axis_size("slide")
    bits = tiles.bit_length() - 1
    in_channels, _, channels = fine_kernel.shape
    classes = class_kernel.shape[0]
    fine, coarse, labels = fine_level[0], coarse_level[0], tissue_labels[0]
    height, width = fine.shape[0], fine.shape[1]
    fine_number = height * tiles * width * (channels // GROUPS)
    numbers = (float(fine_number), float(fine_number // 4))
    pixels, half = height * width, width // 2
    tile_ends, slide_ends = tiles - 1, max(slides - 1, 1)
    chunk = in_channels // tiles
    row_count = -(-(5 + classes) // 8) * 8

    inputs = dict(
        fine=fine,
        coarse=coarse,
        fine_taps=fine_kernel.transpose(1, 0, 2),
        coarse_taps=coarse_kernel.transpose(1, 0, 2),
        fine_gain=fine_gain[None, :],
        fine_offset=fine_offset[None, :],
        coarse_gain=coarse_gain[None, :],
        coarse_offset=coarse_offset[None, :],
        class_kernel=class_kernel,
        class_offset=class_offset[None, :],
        labels=labels,
    )
    outputs = dict(
        final=shape_of((slides, chunk, 18 * channels)),
        head_gather=shape_of((slides, row_count, channels)),
        total_out=shape_of((1, channels)),
    )
    line = (1, channels)
    scratch = dict(
        fine_pad=pltpu.VMEM((height + 2, width, in_channels), BF16),
        coarse_pad=pltpu.VMEM((height // 2 + 2, half, in_channels), BF16),
        fine_conv=pltpu.VMEM((pixels, channels), F32),
        coarse_conv=pltpu.VMEM((pixels // 4, channels), F32),
        fine_dpre=pltpu.VMEM((pixels, channels), F32),
        coarse_dpre=pltpu.VMEM((pixels // 4, channels), F32),
        fine_turned=pltpu.VMEM((in_channels, (height + 2) * width), BF16),
        coarse_turned=pltpu.VMEM((in_channels, (height // 2 + 2) * half), BF16),
        fine_shifted=pltpu.VMEM((pixels, 3 * channels), BF16),
        coarse_shifted=pltpu.VMEM((pixels // 4, 3 * channels), BF16),
        widen=pltpu.VMEM((width, channels), F32),
        fold=pltpu.VMEM((width, channels), F32),
        sums=pltpu.VMEM((8, channels), F32),
        rows=pltpu.VMEM((row_count, channels), F32),
        slide_rows=pltpu.VMEM((row_count, channels), F32),
        row_gather=pltpu.VMEM((tiles, row_count, channels), F32),
        count=pltpu.VMEM(line, F32),
        stat=pltpu.VMEM(line, F32),
        back=pltpu.VMEM(line, F32),
        slide_count=pltpu.VMEM(line, F32),
        count_gather=pltpu.VMEM((tiles,) + line, F32),
        stat_gather=pltpu.VMEM((tiles,) + line, F32),
        back_gather=pltpu.VMEM((tiles,) + line, F32),
        total_gather=pltpu.VMEM((slides,) + line, F32),
        edge_send=dma_sems(2, 2),
        edge_recv=dma_sems(2, 2),
        tile_send=dma_sems(4, tile_ends),
        tile_recv=dma_sems(4, tile_ends),
        slide_send=dma_sems(6, slide_ends),
        slide_recv=dma_sems(6, slide_ends),
        stage_send=dma_sems(4, bits),
        stage_recv=dma_sems(4, bits),
    )
    parts = {}
    for piece in range(4):
        span = 9 * channels if piece == 0 else 3 * channels
        parts[GRAD, piece, 0] = pltpu.VMEM((2,) * bits + (chunk, span), F32)
        plan = stage_plan(bits, order_of(bits, piece % 2 == 0))
        for stage, (_, _, left) in enumerate(plan):
            below = (2,) * left + (chunk, span)
            parts[RECV, piece, stage] = pltpu.VMEM(below, BF16 if stage else F32)
            if stage:
                parts[SEND, piece, stage] = pltpu.VMEM(below, BF16)
                parts[KEPT, piece, stage] = pltpu.VMEM(below, F32)
    names = list(inputs) + list(outputs) + list(scratch)
    final, heads, total = call(
        functools.partial(step_kernel, tiles, slides, bits, numbers, names, list(parts)),
        tuple(outputs.values()),
        list(scratch.values()) + list(parts.values()),
        tuple(inputs.values()),
        0,
    )
    loss, head, grads = call(
        functools.partial(finish_kernel, slides, classes),
        (
            shape_of((1, 1)),
            shape_of((4 + classes, channels)),
            shape_of((chunk, 9, 2, channels)),
        ),
        [],
        (final, heads, total),
    )
    return (loss[0, 0], head, grads.transpose(0, 2, 1, 3))


def solution(mesh):
    return jax.shard_map(
        per_device,
        mesh=mesh,
        in_specs=(
            P("slide", "tile", None, None),
            P("slide", "tile", None, None),
            P(),
            P(),
            P(),
            P(),
            P(),
            P(),
            P(),
            P(),
            P("slide", "tile", None),
        ),
        out_specs=(P(), P(), P("tile", None, None, None)),
        check_vma=False,
    )
```

```python
import functools
import types

import jax
import jax.numpy as jnp
from jax import lax
from jax.experimental import pallas as pl
from jax.experimental.pallas import tpu as pltpu
from jax.sharding import PartitionSpec as P

GROUPS = 32
EPSILON = 1e-05
F32 = jnp.float32
BF16 = jnp.bfloat16
MESH = pl.DeviceIdType.MESH
VMEM = pl.BlockSpec(memory_space=pltpu.VMEM)
LIMIT = 60 * 1024 * 1024
HIGH = lax.Precision.HIGHEST


def call(body, out_shape, scratch, args, collective_id=None):
    if collective_id is None:
        params = pltpu.CompilerParams(vmem_limit_bytes=LIMIT)
    else:
        params = pltpu.CompilerParams(
            vmem_limit_bytes=LIMIT, collective_id=collective_id, has_side_effects=True
        )
    return pl.pallas_call(
        body,
        out_shape=out_shape,
        in_specs=[VMEM] * len(args),
        out_specs=jax.tree.map(lambda _: VMEM, out_shape),
        scratch_shapes=scratch,
        compiler_params=params,
    )(*args)


def shape_of(dims, dtype=F32):
    return jax.ShapeDtypeStruct(dims, dtype)


def greet(peers, meanwhile):
    barrier = pltpu.get_barrier_semaphore()
    for peer in peers:
        pl.semaphore_signal(barrier, inc=1, device_id=peer, device_id_type=MESH)
    meanwhile()
    pl.semaphore_wait(barrier, len(peers))


def ring_peers(axis, size):
    me = lax.axis_index(axis)
    return [{axis: lax.rem(me + d, size)} for d in range(1, size)]


def spread_copies(axis, size, source, gather, send_sem, recv_sem):
    me = lax.axis_index(axis)
    return [
        pltpu.make_async_remote_copy(
            src_ref=source,
            dst_ref=gather.at[me],
            send_sem=send_sem.at[d - 1],
            recv_sem=recv_sem.at[d - 1],
            device_id={axis: lax.rem(me + d, size)},
            device_id_type=MESH,
        )
        for d in range(1, size)
    ]


def ordered_sum(gather, size):
    total = gather[0]
    for index in range(1, size):
        total = total + gather[index]
    return total


def dma_sems(*dims):
    return pltpu.SemaphoreType.DMA(dims)


def column_of(shape, width):
    return lax.rem(lax.broadcasted_iota(jnp.int32, shape, 0), width)


def from_left(values, width):
    moved = pltpu.roll(values, 1, axis=0)
    return jnp.where(column_of(values.shape, width) == 0, 0.0, moved)


def from_right(values, width):
    moved = pltpu.roll(values, values.shape[0] - 1, axis=0)
    return jnp.where(column_of(values.shape, width) == width - 1, 0.0, moved)


def stage_plan(bits, order):
    left = list(reversed(range(bits)))
    plan = []
    for bit in order:
        place = left.index(bit)
        left = [other for other in left if other != bit]
        plan.append((bit, place, len(left)))
    return plan


def at_bits(places, count):
    index = [slice(None)] * count
    for place, value in places:
        index[place] = value
    return tuple(index)


def order_of(bits, turn):
    order = list(range(bits))
    if turn and bits > 2:
        order[1], order[2] = order[2], order[1]
    return order


def lanes_of(shape, dim=1):
    return lax.broadcasted_iota(jnp.int32, shape, dim)


def packed_groups(rows, channels):
    shape = (channels, channels)
    member = lanes_of(shape, 0) // (channels // GROUPS) == lax.rem(lanes_of(shape), GROUPS)
    sums = jnp.dot(rows, member.astype(F32), preferred_element_type=F32, precision=HIGH)
    own = lanes_of(rows.shape) // GROUPS == lanes_of(rows.shape, 0)
    return jnp.sum(jnp.where(own, sums, 0.0), axis=0, keepdims=True)


def unpacked_groups(row, channels):
    shape = (channels, channels)
    member = lax.rem(lanes_of(shape, 0), GROUPS) == lanes_of(shape) // (channels // GROUPS)
    own = lanes_of((8, channels)) // GROUPS == lanes_of((8, channels), 0)
    rows = jnp.where(own, jnp.broadcast_to(row, (8, channels)), 0.0)
    return jnp.dot(rows, member.astype(F32), preferred_element_type=F32, precision=HIGH)


PACK = 2
PIECES = 6
GRAD, SEND, RECV, KEPT = range(4)


def conv_step(step, padded, taps, out, sums, at):
    width, depth = padded.shape[1], padded.shape[2]
    channels = taps.shape[2]
    size = PACK * width
    total = None
    for a in range(3):
        block = padded[pl.ds(step * PACK + a, PACK)].reshape(size, depth)
        side = jnp.concatenate([taps[3 * a + b] for b in range(3)], axis=1)
        term = jnp.dot(block, side, preferred_element_type=F32)
        total = term if total is None else total + term
    value = (
        from_left(total[:, :channels], width)
        + total[:, channels : 2 * channels]
        + from_right(total[:, 2 * channels :], width)
    )
    here = step * size if isinstance(step, int) else pl.multiple_of(step * size, size)
    out[pl.ds(here, size), :] = value
    sums[at : at + 1] += jnp.sum(value, axis=0, keepdims=True)
    sums[at + 1 : at + 2] += jnp.sum(value * value, axis=0, keepdims=True)


def step_kernel(tiles, slides, bits, numbers, names, keys, *refs):
    ref = types.SimpleNamespace(**dict(zip(names, refs)))
    ref.parts = dict(zip(keys, refs[len(names) :]))
    fine, coarse, labels = ref.fine, ref.coarse, ref.labels
    fine_pad, coarse_pad = ref.fine_pad, ref.coarse_pad
    fine_conv, coarse_conv = ref.fine_conv, ref.coarse_conv
    sums, rows, class_kernel = ref.sums, ref.rows, ref.class_kernel
    me, slide = lax.axis_index("tile"), lax.axis_index("slide")
    height, width, _ = fine.shape
    channels = fine_conv.shape[1]
    classes = class_kernel.shape[0]
    fine_gain, fine_offset = ref.fine_gain[...], ref.fine_offset[...]
    coarse_gain, coarse_offset = ref.coarse_gain[...], ref.coarse_offset[...]

    def prepare():
        tissue_here = (labels[...] >= 0).astype(F32)
        ref.count[...] = jnp.broadcast_to(
            jnp.sum(tissue_here, axis=(0, 1), keepdims=True), ref.count.shape
        )
        sums[...] = jnp.zeros_like(sums)
        fine_pad[pl.ds(1, height)] = fine[...]
        coarse_pad[pl.ds(1, height // 2)] = coarse[...]

    greet(ring_peers("tile", tiles) + ring_peers("slide", slides), prepare)

    def edge_copies(peer, down):
        return [
            pltpu.make_async_remote_copy(
                src_ref=source.at[source.shape[0] - 1 if down else 0],
                dst_ref=target.at[0 if down else target.shape[0] - 1],
                send_sem=ref.edge_send.at[int(down), at],
                recv_sem=ref.edge_recv.at[int(down), at],
                device_id={"tile": peer},
                device_id_type=MESH,
            )
            for at, (source, target) in enumerate(((fine, fine_pad), (coarse, coarse_pad)))
        ]

    down = edge_copies(lax.rem(me + 1, tiles), True)
    up = edge_copies(lax.rem(me + tiles - 1, tiles), False)

    @pl.when(me < tiles - 1)
    def _():
        for copy in down:
            copy.start()

    @pl.when(me > 0)
    def _():
        for copy in up:
            copy.start()

    def tile_copies(at, source, gather):
        return spread_copies(
            "tile", tiles, source, gather, ref.tile_send.at[at], ref.tile_recv.at[at]
        )

    def slide_copies(at, source, gather):
        return spread_copies(
            "slide", slides, source, gather, ref.slide_send.at[at], ref.slide_recv.at[at]
        )

    def start(copies):
        for copy in copies:
            copy.start()

    def wait(copies):
        for copy in copies:
            copy.wait()

    counts = tile_copies(0, ref.count, ref.count_gather)
    start(counts)
    ref.count_gather[me] = ref.count[...]

    @pl.when(me == 0)
    def _():
        for padded in (fine_pad, coarse_pad):
            padded[0] = jnp.zeros(padded.shape[1:], BF16)

    @pl.when(me == tiles - 1)
    def _():
        for padded in (fine_pad, coarse_pad):
            padded[padded.shape[0] - 1] = jnp.zeros(padded.shape[1:], BF16)

    fine_steps, coarse_steps = height // PACK, height // 2 // PACK

    @pl.loop(1, fine_steps - 1)
    def _(step):
        conv_step(step, fine_pad, ref.fine_taps, fine_conv, sums, 0)

    @pl.when(me < tiles - 1)
    def _():
        for copy in down:
            copy.wait_send()
        for copy in up:
            copy.wait_recv()

    @pl.when(me > 0)
    def _():
        for copy in up:
            copy.wait_send()
        for copy in down:
            copy.wait_recv()

    @pl.loop(0, 2)
    def _(side):
        conv_step(side * (fine_steps - 1), fine_pad, ref.fine_taps, fine_conv, sums, 0)

    @pl.loop(0, coarse_steps)
    def _(step):
        conv_step(step, coarse_pad, ref.coarse_taps, coarse_conv, sums, 2)

    ref.stat[...] = packed_groups(sums[...], channels)
    stat_copies = tile_copies(1, ref.stat, ref.stat_gather)
    start(stat_copies)
    wait(counts)
    ref.slide_count[...] = ordered_sum(ref.count_gather, tiles)
    total_copies = slide_copies(0, ref.slide_count, ref.total_gather)
    start(total_copies)
    ref.stat_gather[me] = ref.stat[...]
    ref.total_gather[slide] = ref.slide_count[...]

    for padded, turned in ((fine_pad, ref.fine_turned), (coarse_pad, ref.coarse_turned)):
        span = padded.shape[1]
        for row in range(padded.shape[0]):
            turned[:, row * span : (row + 1) * span] = padded[row].T

    wait(stat_copies)
    wait(total_copies)
    total = ordered_sum(ref.total_gather, slides)
    count = total[0:1, 0:1]
    ref.total_out[...] = total
    group_sums = unpacked_groups(ordered_sum(ref.stat_gather, tiles), channels)

    def terms_of(at, number):
        mean = group_sums[at : at + 1] / number
        variance = group_sums[at + 1 : at + 2] / number - mean * mean
        return mean, lax.rsqrt(variance + EPSILON)

    fine_mean, fine_scale = terms_of(0, numbers[0])
    coarse_mean, coarse_scale = terms_of(2, numbers[1])

    size, half = 2 * width, width // 2
    square = (classes, classes)
    offset = jnp.sum(
        jnp.where(
            lanes_of(square) == lanes_of(square, 0),
            jnp.broadcast_to(ref.class_offset[...], square),
            0.0,
        ),
        axis=1,
        keepdims=True,
    )
    rows[...] = jnp.zeros_like(rows)
    widen, fold = ref.widen, ref.fold
    fine_dpre, coarse_dpre = ref.fine_dpre, ref.coarse_dpre

    @pl.loop(0, height // 2)
    def _(step):
        fine_at = pl.ds(pl.multiple_of(step * size, size), size)
        coarse_at = pl.ds(pl.multiple_of(step * half, half), half)
        fine_normed = (fine_conv[fine_at, :] - fine_mean) * fine_scale
        fine_pre = fine_normed * fine_gain + fine_offset
        coarse_normed = (coarse_conv[coarse_at, :] - coarse_mean) * coarse_scale
        coarse_pre = coarse_normed * coarse_gain + coarse_offset
        coarse_act = jnp.maximum(coarse_pre, 0.0)
        widen[pl.ds(0, half, stride=2), :] = coarse_act
        widen[pl.ds(1, half, stride=2), :] = coarse_act
        upsampled = widen[...]
        merged = (
            jnp.maximum(fine_pre, 0.0) + jnp.concatenate([upsampled, upsampled], axis=0)
        ).astype(BF16)
        logits = (
            lax.dot_general(
                class_kernel[...], merged, (((1,), (1,)), ((), ())), preferred_element_type=F32
            )
            + offset
        )
        label = jnp.concatenate(
            [labels[pl.ds(2 * step, 1), :], labels[pl.ds(2 * step + 1, 1), :]], axis=1
        )
        onehot = (lanes_of((classes, size), 0) == label).astype(F32)
        tissue = (label >= 0).astype(F32)
        top = jnp.max(logits, axis=0, keepdims=True)
        lse = top + jnp.log(jnp.sum(jnp.exp(logits - top), axis=0, keepdims=True))
        picked = jnp.sum(onehot * logits, axis=0, keepdims=True)
        loss = jnp.sum((lse - picked) * tissue, axis=1, keepdims=True)
        dlogits = ((jnp.exp(logits - lse) - onehot) * tissue / count).astype(BF16)
        dmerged = lax.dot_general(
            dlogits, class_kernel[...], (((0,), (0,)), ((), ())), preferred_element_type=F32
        )
        fine_d = jnp.where(fine_pre > 0, dmerged, 0.0)
        fine_dpre[fine_at, :] = fine_d
        fold[...] = dmerged[:width] + dmerged[width:]
        blocks = fold[pl.ds(0, half, stride=2), :] + fold[pl.ds(1, half, stride=2), :]
        coarse_d = jnp.where(coarse_pre > 0, blocks, 0.0)
        coarse_dpre[coarse_at, :] = coarse_d
        rows[0:1] += jnp.sum(fine_d * fine_normed, axis=0, keepdims=True)
        rows[1:2] += jnp.sum(fine_d, axis=0, keepdims=True)
        rows[2:3] += jnp.sum(coarse_d * coarse_normed, axis=0, keepdims=True)
        rows[3:4] += jnp.sum(coarse_d, axis=0, keepdims=True)
        rows[4 : 4 + classes] += jnp.dot(dlogits, merged, preferred_element_type=F32)
        rows[4 + classes : 5 + classes] += jnp.broadcast_to(loss, (1, channels))

    gains = jnp.concatenate([fine_gain, fine_gain, coarse_gain, coarse_gain] * 2, axis=0)
    ref.back[...] = packed_groups(rows[0:8] * gains, channels)
    back_copies = tile_copies(2, ref.back, ref.back_gather)
    start(back_copies)
    ref.back_gather[me] = ref.back[...]
    ref.row_sums[0] = rows[...]
    wait(back_copies)
    back = unpacked_groups(ordered_sum(ref.back_gather, tiles), channels)

    def upstream(conv, dpre, mean, scale, gain, at, number, span, shifted, steps):
        first = back[at + 1 : at + 2] / number
        second = back[at : at + 1] / number
        block = PACK * span

        @pl.loop(0, steps)
        def _(step):
            here = pl.ds(pl.multiple_of(step * block, block), block)
            normed = (conv[here, :] - mean) * scale
            dconv = (dpre[here, :] * gain - first - normed * second) * scale
            shifted[here, :] = jnp.concatenate(
                [
                    from_right(dconv, span).astype(BF16),
                    dconv.astype(BF16),
                    from_left(dconv, span).astype(BF16),
                ],
                axis=1,
            )

    mine = [lax.rem(me // (2**bit), 2) for bit in range(bits)]
    partners = [{"tile": me + (1 - 2 * mine[bit]) * (2**bit)} for bit in range(bits)]
    plans = [stage_plan(bits, order_of(bits, piece % 2)) for piece in range(PIECES)]
    final = ref.final
    across = 3 * channels
    spans = [((piece + 3) % PIECES * across, across) for piece in range(PIECES)]

    def buffer(piece, stage, kind):
        return ref.parts[kind, piece, stage]

    def stage_copy(piece, stage):
        bit, place, left = plans[piece][stage]
        if stage == 0:
            source = ref.parts[GRAD, piece, 0].at[at_bits([(place, 1 - mine[bit])], left + 1)]
        else:
            source = buffer(piece, stage, SEND)
        return pltpu.make_async_remote_copy(
            src_ref=source,
            dst_ref=buffer(piece, stage, RECV),
            send_sem=ref.stage_send.at[piece, stage],
            recv_sem=ref.stage_recv.at[piece, stage],
            device_id=partners[bit],
            device_id_type=MESH,
        )

    def piece_copies(piece):
        lanes = pl.ds(*spans[piece])
        return [
            pltpu.make_async_remote_copy(
                src_ref=final.at[slide, :, lanes],
                dst_ref=final.at[slide, :, lanes],
                send_sem=ref.slide_send.at[2 + piece, d - 1],
                recv_sem=ref.slide_recv.at[2 + piece, d - 1],
                device_id={"slide": lax.rem(slide + d, slides)},
                device_id_type=MESH,
            )
            for d in range(1, slides)
        ]

    done = [0] * PIECES

    def advance(piece):
        stage = done[piece]
        if stage == bits:
            return
        done[piece] += 1
        bit, place, left = plans[piece][stage]
        stage_copy(piece, stage).wait()
        if stage == 0:
            kept = ref.parts[GRAD, piece, 0].at[at_bits([(place, mine[bit])], left + 1)]
        else:
            kept = buffer(piece, stage, KEPT)
        came = buffer(piece, stage, RECV)
        if stage == bits - 1:
            final[slide, :, pl.ds(*spans[piece])] = kept[...] + came[...].astype(F32)
            start(piece_copies(piece))
            return
        later, spot, _ = plans[piece][stage + 1]

        def part(value):
            chosen = at_bits([(spot, value)], left)
            return kept[chosen] + came[chosen].astype(F32)

        buffer(piece, stage + 1, SEND)[...] = part(1 - mine[later]).astype(BF16)
        stage_copy(piece, stage + 1).start()
        buffer(piece, stage + 1, KEPT)[...] = part(mine[later])

    def product(turned, shifted, a, span):
        pixels = shifted.shape[0]
        return jnp.dot(
            turned[:, a * span : a * span + pixels], shifted[...], preferred_element_type=F32
        )

    def row_copy(stage):
        return pltpu.make_async_remote_copy(
            src_ref=ref.row_sums.at[stage],
            dst_ref=ref.row_gather.at[stage],
            send_sem=ref.row_send.at[stage],
            recv_sem=ref.row_recv.at[stage],
            device_id=partners[stage],
            device_id_type=MESH,
        )

    head_copies = slide_copies(1, ref.row_sums.at[bits], ref.head_gather)

    def advance_rows(stage):
        row_copy(stage).wait()
        ref.row_sums[stage + 1] = ref.row_sums[stage] + ref.row_gather[stage]
        if stage + 1 < bits:
            row_copy(stage + 1).start()
        else:
            start(head_copies)
            ref.head_gather[slide] = ref.row_sums[bits]

    def begin(piece, turned, shifted, a, span):
        out = ref.parts[GRAD, piece, 0]
        out[...] = product(turned, shifted, a, span).reshape(out.shape)
        stage_copy(piece, 0).start()

    row_copy(0).start()
    upstream(coarse_conv, coarse_dpre, coarse_mean, coarse_scale, coarse_gain, 2, numbers[1],
             half, ref.coarse_shifted, coarse_steps)
    for a in range(3):
        begin(a, ref.coarse_turned, ref.coarse_shifted, a, half)
    upstream(fine_conv, fine_dpre, fine_mean, fine_scale, fine_gain, 0, numbers[0],
             width, ref.fine_shifted, fine_steps)
    advance(0)
    begin(3, ref.fine_turned, ref.fine_shifted, 0, width)
    advance(1)
    begin(4, ref.fine_turned, ref.fine_shifted, 1, width)
    advance(2)
    begin(5, ref.fine_turned, ref.fine_shifted, 2, width)
    for stage in range(bits):
        for piece in range(PIECES // 2):
            advance(piece)
        advance_rows(stage)
        for piece in range(PIECES // 2, PIECES):
            advance(piece)
    wait(head_copies)
    for piece in range(PIECES):
        wait(piece_copies(piece))


def finish_kernel(slides, classes, final, heads, total, loss, head, grads):
    channels = head.shape[1]
    whole = ordered_sum(final, slides)
    for level in range(2):
        for tap in range(9):
            at = (9 * level + tap) * channels
            grads[:, tap, level, :] = whole[:, at : at + channels]
    rows = ordered_sum(heads, slides)
    head[...] = rows[: 4 + classes]
    loss[...] = rows[4 + classes : 5 + classes, 0:1] / total[0:1, 0:1]


def per_device(
    fine_level,
    coarse_level,
    fine_kernel,
    coarse_kernel,
    fine_gain,
    fine_offset,
    coarse_gain,
    coarse_offset,
    class_kernel,
    class_offset,
    tissue_labels,
):
    tiles, slides = lax.axis_size("tile"), lax.axis_size("slide")
    bits = tiles.bit_length() - 1
    in_channels, _, channels = fine_kernel.shape
    classes = class_kernel.shape[0]
    fine, coarse, labels = fine_level[0], coarse_level[0], tissue_labels[0]
    height, width = fine.shape[0], fine.shape[1]
    fine_number = height * tiles * width * (channels // GROUPS)
    numbers = (float(fine_number), float(fine_number // 4))
    pixels, half = height * width, width // 2
    tile_ends, slide_ends = tiles - 1, max(slides - 1, 1)
    chunk = in_channels // tiles
    row_count = -(-(5 + classes) // 8) * 8

    inputs = dict(
        fine=fine,
        coarse=coarse,
        fine_taps=fine_kernel.transpose(1, 0, 2),
        coarse_taps=coarse_kernel.transpose(1, 0, 2),
        fine_gain=fine_gain[None, :],
        fine_offset=fine_offset[None, :],
        coarse_gain=coarse_gain[None, :],
        coarse_offset=coarse_offset[None, :],
        class_kernel=class_kernel,
        class_offset=class_offset[None, :],
        labels=labels,
    )
    outputs = dict(
        final=shape_of((slides, chunk, 18 * channels)),
        head_gather=shape_of((slides, row_count, channels)),
        total_out=shape_of((1, channels)),
    )
    line = (1, channels)
    scratch = dict(
        fine_pad=pltpu.VMEM((height + 2, width, in_channels), BF16),
        coarse_pad=pltpu.VMEM((height // 2 + 2, half, in_channels), BF16),
        fine_conv=pltpu.VMEM((pixels, channels), F32),
        coarse_conv=pltpu.VMEM((pixels // 4, channels), F32),
        fine_dpre=pltpu.VMEM((pixels, channels), F32),
        coarse_dpre=pltpu.VMEM((pixels // 4, channels), F32),
        fine_turned=pltpu.VMEM((in_channels, (height + 2) * width), BF16),
        coarse_turned=pltpu.VMEM((in_channels, (height // 2 + 2) * half), BF16),
        fine_shifted=pltpu.VMEM((pixels, 3 * channels), BF16),
        coarse_shifted=pltpu.VMEM((pixels // 4, 3 * channels), BF16),
        widen=pltpu.VMEM((width, channels), F32),
        fold=pltpu.VMEM((width, channels), F32),
        sums=pltpu.VMEM((8, channels), F32),
        rows=pltpu.VMEM((row_count, channels), F32),
        row_sums=pltpu.VMEM((bits + 1, row_count, channels), F32),
        row_gather=pltpu.VMEM((bits, row_count, channels), F32),
        row_send=dma_sems(bits),
        row_recv=dma_sems(bits),
        count=pltpu.VMEM(line, F32),
        stat=pltpu.VMEM(line, F32),
        back=pltpu.VMEM(line, F32),
        slide_count=pltpu.VMEM(line, F32),
        count_gather=pltpu.VMEM((tiles,) + line, F32),
        stat_gather=pltpu.VMEM((tiles,) + line, F32),
        back_gather=pltpu.VMEM((tiles,) + line, F32),
        total_gather=pltpu.VMEM((slides,) + line, F32),
        edge_send=dma_sems(2, 2),
        edge_recv=dma_sems(2, 2),
        tile_send=dma_sems(3, tile_ends),
        tile_recv=dma_sems(3, tile_ends),
        slide_send=dma_sems(2 + PIECES, slide_ends),
        slide_recv=dma_sems(2 + PIECES, slide_ends),
        stage_send=dma_sems(PIECES, bits),
        stage_recv=dma_sems(PIECES, bits),
    )
    parts = {}
    span = 3 * channels
    for piece in range(PIECES):
        parts[GRAD, piece, 0] = pltpu.VMEM((2,) * bits + (chunk, span), F32)
        plan = stage_plan(bits, order_of(bits, piece % 2))
        for stage, (_, _, left) in enumerate(plan):
            below = (2,) * left + (chunk, span)
            parts[RECV, piece, stage] = pltpu.VMEM(below, BF16 if stage else F32)
            if stage:
                parts[SEND, piece, stage] = pltpu.VMEM(below, BF16)
                parts[KEPT, piece, stage] = pltpu.VMEM(below, F32)
    names = list(inputs) + list(outputs) + list(scratch)
    final, heads, total = call(
        functools.partial(step_kernel, tiles, slides, bits, numbers, names, list(parts)),
        tuple(outputs.values()),
        list(scratch.values()) + list(parts.values()),
        tuple(inputs.values()),
        0,
    )
    loss, head, grads = call(
        functools.partial(finish_kernel, slides, classes),
        (
            shape_of((1, 1)),
            shape_of((4 + classes, channels)),
            shape_of((chunk, 9, 2, channels)),
        ),
        [],
        (final, heads, total),
    )
    return (loss[0, 0], head, grads.transpose(0, 2, 1, 3))


def solution(mesh):
    return jax.shard_map(
        per_device,
        mesh=mesh,
        in_specs=(
            P("slide", "tile", None, None),
            P("slide", "tile", None, None),
            P(),
            P(),
            P(),
            P(),
            P(),
            P(),
            P(),
            P(),
            P("slide", "tile", None),
        ),
        out_specs=(P(), P(), P("tile", None, None, None)),
        check_vma=False,
    )
```
